32 devices in a mesh: groups: 2 (over x), seq: 4 (over z), expert: 4 (over y, core).
Axes of the slice: x: 2, y: 2, z: 4, core: 2. Of those that a mesh axis runs over, the one named last changes fastest.
Arguments:
- q_lat: bfloat16 [512, 65536], P(('groups', 'seq'), 'expert'), parts along dimension 0, may hold values from -36 to 36
- q_rope: bfloat16 [512, 8192], P(('groups', 'seq'), 'expert'), parts along dimension 0, may hold values from -6 to 6
- cache_lat: bfloat16 [2048, 512], P(('groups', 'seq')), parts along dimension 0, may hold values from -7 to 7
- cache_rope: bfloat16 [2048, 64], P(('groups', 'seq')), parts along dimension 0, may hold values from -8 to 8
- tool_lat: bfloat16 [256, 512], P(('groups', 'seq')), parts along dimension 0, may hold values from -2.5 to 2.5
- tool_rope: bfloat16 [256, 64], P(('groups', 'seq')), parts along dimension 0, may hold values from -8 to 8
- offset: int32 [2], P('groups'), parts along dimension 0, may hold values from 512 to 736
- suf_lat: bfloat16 [512, 512], P(('groups', 'seq')), parts along dimension 0, may hold values from -6 to 6
- suf_rope: bfloat16 [512, 64], P(('groups', 'seq')), parts along dimension 0, may hold values from -8 to 8
- w_uv: bfloat16 [128, 512, 128], P('expert'), may hold values from -1 to 1
- w_out: bfloat16 [16384, 7168], P('expert', 'seq'), may hold values from -0.19921875 to 0.19921875
- resid: bfloat16 [512, 7168], P(('groups', 'expert'), 'seq'), parts along dimension 0, may hold values from -36 to 36
- routes: int32 [512, 2], P(('groups', 'expert')), parts along dimension 0, may hold values from 0 to 3, all different within a row; in each aligned block of 64 rows (0 to 63, 64 to 127, ...) at most 40 rows name the same one
- probs: float32 [512, 2], P(('groups', 'expert')), parts along dimension 0, may hold values from 0.1 to 1
- w_gate: bfloat16 [4, 7168, 1024], P('expert', None, 'seq'), may hold values from -0.0625 to 0.0625
- w_up: bfloat16 [4, 7168, 1024], P('expert', None, 'seq'), may hold values from -0.0625 to 0.0625
- w_down: bfloat16 [4, 1024, 7168], P('expert', 'seq'), may hold values from -0.1875 to 0.1875
Outputs:
- attn_residual: bfloat16 [512, 7168], P(('groups', 'expert'), 'seq'), parts along dimension 0
- expert_mix: bfloat16 [512, 7168], P(('groups', 'expert'), 'seq'), parts along dimension 0
The draws below stay inside these ranges and needn't reach their ends.
There are 2 independent parts, one for each index of `groups`. The reference program is written for one: setup_inputs(seed, part) draws one part's arguments, and reference() takes and returns one part's arrays. A program takes and returns all parts, laid end to end along the dimension named above; an argument that names none is the same for every part. Nothing has to cross between parts.
Inputs may be any that keep to these rules, and one draw needn't show every extreme that they name: `routes`: within the rows of one device of the expert axis (64 rows in a row), no expert is named more than 40 times.
All inputs are finite; a program needn't handle non-finite values.
Results may differ from the reference program's by a relative error of at most 0.03.
Values may be sent and summed in bfloat16 or wider, within the bound.
No kernel may reach another device: no remote copies, remote signals or barrier semaphores. Data moves between devices by JAX's collectives and lax.ppermute only.
A program may use at most 128 MiB of HBM per device.

```python
import math
import jax
import jax.numpy as jnp
import numpy as np
from jax import lax

D = 7168
H = 128
LAT = 512
ROPE = 64
VDIM = 128
FF_EXP = 1024
CTX_DEV = 256
TOOL_DEV = 32
SUF = 256
CTX = 1024
TOOL = 128
TE = 64
EXPERTS = 4
TOP = 2
CAP = 40
N_SEQ = 4


def base_latents(key):
    return jnp.clip(jax.random.normal(jax.random.fold_in(key, 101), (CTX, LAT), jnp.float32), -6.0, 6.0)


def draw_cache_lat(key, part):
    latents = base_latents(key)
    return latents.astype(jnp.bfloat16)


def draw_q_lat(key, part):
    queries = jnp.clip(jax.random.normal(jax.random.fold_in(key, 104), (SUF, H * LAT), jnp.float32), -6.0, 6.0)
    return queries.astype(jnp.bfloat16)


def draw_resid(key, part):
    row_scale = jnp.exp(jax.random.uniform(jax.random.fold_in(key, 107), (SUF, 1), jnp.float32, jnp.log(0.3), jnp.log(3.0)))
    rise = jnp.sqrt(3.0) ** (jnp.arange(D, dtype=jnp.float32) / D)
    column_scale = rise * jax.random.uniform(jax.random.fold_in(key, 108), (D,), jnp.float32, 0.6, 1.4)
    values = jnp.clip(jax.random.normal(jax.random.fold_in(key, 109), (SUF, D), jnp.float32), -4.0, 4.0)
    return (0.5 * row_scale * column_scale[None, :] * values).astype(jnp.bfloat16)


def block_levels(key, shape, shards, least, top_value):
    level, own = 1.0, jax.random.fold_in(key, 6)
    for axis_at, parts in shards:
        heights = jnp.exp(jax.random.uniform(jax.random.fold_in(own, axis_at), (parts,), jnp.float32, least / len(shards), top_value / len(shards)))
        level = level * jnp.repeat(heights, shape[axis_at] // parts).reshape([-1 if axis == axis_at else 1 for axis in range(len(shape))])
    return level


def assign_block(stream_key, own, number, rows, number_of, top, limit, slope):
    order = jax.random.permutation(stream_key, number_of)
    crowded, ordinary = portions_of(number_of, rows * top, limit, slope, True), portions_of(number_of, rows * top, limit, slope, False)
    places = jnp.arange(number_of)

    def named(sizes, offset_by):
        used = int((sizes > 0).sum())
        fixed = max(1, used // 4)
        moved = fixed + (places - fixed + offset_by * (used - fixed)) % max(1, number_of - fixed)
        return jnp.zeros((number_of,), jnp.int32).at[order[jnp.where(places < fixed, places, moved)]].set(jnp.asarray(sizes, jnp.int32))

    sizes = jnp.where(number % 4 == 0, named(crowded, number // 4), named(ordinary, number - number // 4 - 1))
    mixed = jax.random.permutation(jax.random.fold_in(own, 3), number_of)
    donor, taker = mixed[0:number_of // 2 * 2:2], mixed[1:number_of // 2 * 2:2]
    room = jnp.minimum(sizes[donor] - 1, limit - sizes[taker]) // 2
    room = jnp.where((donor == order[0]) | (taker == order[0]) | (sizes[taker] == 0), 0, jnp.maximum(room, 0))
    moved = jax.random.randint(jax.random.fold_in(own, 4), (number_of // 2,), 0, 1 << 20) % (room + 1)
    sizes = sizes.at[donor].add(-moved).at[taker].add(moved)
    items = jnp.searchsorted(jnp.cumsum(sizes), jnp.arange(rows * top), side="right").astype(jnp.int32)
    grid = items.reshape(top, rows).T
    grid = grid[jax.random.permutation(jax.random.fold_in(own, 1), rows)]
    offset_by = jax.random.randint(jax.random.fold_in(own, 2), (rows, 1), 0, top)
    return jnp.take_along_axis(grid, (jnp.arange(top)[None, :] + offset_by) % top, axis=1)


def portions_of(number_of, total, most, slope, full):
    weights = [(1 << 20) // math.isqrt(grade ** slope) + 1 for grade in range(1, number_of + 1)]
    largest = most if full else min(most, max(-(-total // number_of), total * weights[0] // sum(weights)))
    least = 1 if total - largest >= number_of - 1 else 0
    given, rest = [largest] + [least] * (number_of - 1), total - largest - least * (number_of - 1)
    while rest > 0:
        free = [i for i in range(1, number_of) if given[i] < largest] or [i for i in range(1, number_of) if given[i] < most]
        whole, remaining = sum([weights[i] for i in free]), rest
        for i in free:
            extra = min(most - given[i], max(1, remaining * weights[i] // whole), rest)
            given[i] = given[i] + extra
            rest = rest - extra
    return np.array(given)


def scatter_about(rng, shape, deviation, most, split=(), kind=jnp.bfloat16):
    factor_of = block_levels(rng, shape, split, -0.22, 0.18) if split else 1.0
    result = jax.random.normal(rng, shape, jnp.float32) * deviation * factor_of
    return jnp.minimum(jnp.maximum(result, -most), most).astype(kind)


def setup_inputs(seed: int = 0, part: int = 0) -> dict:
    arg_keys = jax.random.split(jax.random.key(seed), 18)
    own_keys = jax.random.split(jax.random.fold_in(arg_keys[17], part), 18)
    q_lat = draw_q_lat(jax.random.fold_in(jax.random.fold_in(arg_keys[17], part), 71), part)
    q_rope = scatter_about(own_keys[1], (SUF, H * ROPE), 1.0, 6.0, ((0, 4), (1, 4)))
    cache_lat = draw_cache_lat(jax.random.fold_in(jax.random.fold_in(arg_keys[17], part), 71), part)
    cache_rope = scatter_about(own_keys[3], (CTX, ROPE), (12 * ROPE ** -0.5), 8.0, ((0, 4),))
    tool_lat = scatter_about(own_keys[4], (TOOL, LAT), (10 * LAT ** -0.5), 2.5, ((0, 4),))
    tool_rope = scatter_about(own_keys[5], (TOOL, ROPE), (12 * ROPE ** -0.5), 8.0, ((0, 4),))
    offset = jax.random.randint(own_keys[6], (1,), CTX // 2, CTX // 2 + CTX_DEV - TOOL_DEV + 1).astype(jnp.int32)
    suf_lat = scatter_about(own_keys[7], (SUF, LAT), 1.0, 6.0, ((0, 4),))
    suf_rope = scatter_about(own_keys[8], (SUF, ROPE), (12 * ROPE ** -0.5), 8.0, ((0, 4),))
    w_uv = scatter_about(arg_keys[9], (H, LAT, VDIM), 0.15, 1.0, ((0, 4),))
    w_out = scatter_about(arg_keys[10], (H * VDIM, D), 0.03, 0.19921875, ((0, 4), (1, 4)))
    resid = draw_resid(jax.random.fold_in(jax.random.fold_in(arg_keys[17], part), 71), part)
    routes_keys = jax.random.split(jax.random.fold_in(own_keys[12], 1), SUF // TE)
    routes_turns = jax.random.permutation(jax.random.fold_in(own_keys[12], 3), SUF // TE)
    routes = jax.vmap(lambda own, number: assign_block(jax.random.fold_in(own_keys[12], 2), own, number, TE, EXPERTS, TOP, CAP, 1))(routes_keys, routes_turns).reshape((SUF, TOP))
    probs = jnp.clip(0.1 + 0.9 * jax.random.uniform(own_keys[13], (SUF, TOP), jnp.float32) ** block_levels(own_keys[13], (SUF, TOP), ((0, 4),), -0.2, 0.2), 0.1, 1.0)
    w_gate = scatter_about(arg_keys[14], (EXPERTS, D, FF_EXP), D ** -0.5, 0.0625, ((0, 4), (2, 4)))
    w_up = scatter_about(arg_keys[15], (EXPERTS, D, FF_EXP), D ** -0.5, 0.0625, ((0, 4), (2, 4)))
    w_down = scatter_about(arg_keys[16], (EXPERTS, FF_EXP, D), FF_EXP ** -0.5, 0.1875, ((0, 4), (1, 4)))
    return {"q_lat": q_lat, "q_rope": q_rope, "cache_lat": cache_lat, "cache_rope": cache_rope, "tool_lat": tool_lat, "tool_rope": tool_rope, "offset": offset, "suf_lat": suf_lat, "suf_rope": suf_rope, "w_uv": w_uv, "w_out": w_out, "resid": resid, "routes": routes, "probs": probs, "w_gate": w_gate, "w_up": w_up, "w_down": w_down}


score_scale = 192.0 ** (-0.5)

def insert_tool(cache, tool, offset):
    position = jnp.arange(cache.shape[0], dtype=jnp.int32)
    shifted = position - offset[0]
    inside = (shifted >= 0) & (shifted < tool.shape[0])
    safe = jnp.clip(shifted, 0, tool.shape[0] - 1).astype(jnp.int32)
    return jnp.where(inside[:, None], jnp.take(tool, safe, axis=0), cache)

def reference(q_lat, q_rope, cache_lat, cache_rope, tool_lat, tool_rope, offset, suf_lat, suf_rope, w_uv, w_out, resid, routes, probs, w_gate, w_up, w_down):
    key_lat = jnp.concatenate([insert_tool(cache_lat, tool_lat, offset), suf_lat], axis=0)
    key_rope = jnp.concatenate([insert_tool(cache_rope, tool_rope, offset), suf_rope], axis=0)
    query_pos = jnp.arange(SUF, dtype=jnp.int32)
    key_pos = jnp.arange(CTX + SUF, dtype=jnp.int32)
    visible = (key_pos[None, :] < CTX) | (key_pos[None, :] - CTX <= query_pos[:, None])
    lat_heads = q_lat.reshape(SUF, H, LAT).transpose(1, 0, 2)
    rope_heads = q_rope.reshape(SUF, H, ROPE).transpose(1, 0, 2)

    def one_head(operands):
        query_lat, query_rope, value_proj = operands
        scores = jnp.dot(query_lat, key_lat.T, preferred_element_type=jnp.float32)
        scores = (scores + jnp.dot(query_rope, key_rope.T, preferred_element_type=jnp.float32)) * score_scale
        scores = jnp.where(visible, scores, -jnp.inf)
        highest = lax.optimization_barrier(jnp.max(scores, axis=1, keepdims=True))
        weights = jnp.where(visible, jnp.exp(scores - highest), 0.0)
        total = lax.optimization_barrier(jnp.sum(weights, axis=1, keepdims=True))
        latent_out = (jnp.dot(weights.astype(jnp.bfloat16), key_lat, preferred_element_type=jnp.float32) / total).astype(jnp.bfloat16)
        return jnp.dot(latent_out, value_proj, preferred_element_type=jnp.float32).astype(jnp.bfloat16)
    values = lax.map(one_head, (lat_heads, rope_heads, w_uv))
    values = values.transpose(1, 0, 2).reshape(SUF, H * VDIM)
    attn_residual = (resid.astype(jnp.float32) + jnp.dot(values, w_out, preferred_element_type=jnp.float32)).astype(jnp.bfloat16)
    stream = attn_residual.astype(jnp.float32)
    normed = (stream * lax.rsqrt(lax.optimization_barrier(jnp.mean(stream * stream, axis=1, keepdims=True)) + 1e-06)).astype(jnp.bfloat16)
    route_weight = 2.5 * probs / lax.optimization_barrier(jnp.sum(probs, axis=1, keepdims=True))
    block_units = FF_EXP // N_SEQ

    def one_expert(mixed, operands):
        gate_proj, up_proj, down_proj, expert_id = operands
        gate = jnp.dot(normed, gate_proj, preferred_element_type=jnp.float32)
        upper = jnp.dot(normed, up_proj, preferred_element_type=jnp.float32)
        inner = (jax.nn.silu(gate) * upper).astype(jnp.bfloat16)
        blocks = jnp.einsum('tsf,sfd->tsd', inner.reshape(SUF, N_SEQ, block_units).astype(jnp.float32), down_proj.reshape(N_SEQ, block_units, D).astype(jnp.float32))
        rounded = lax.optimization_barrier(blocks.astype(jnp.bfloat16))
        summed = lax.optimization_barrier(jnp.sum(rounded.astype(jnp.float32), axis=1))
        expert_out = lax.optimization_barrier(summed.astype(jnp.bfloat16)).astype(jnp.float32)
        weight = lax.optimization_barrier(jnp.sum(route_weight * (routes == expert_id).astype(jnp.float32), axis=1))
        return (mixed + weight[:, None] * expert_out, None)
    mixed, unused = lax.scan(one_expert, jnp.zeros((SUF, D), jnp.float32), (w_gate, w_up, w_down, jnp.arange(EXPERTS, dtype=jnp.int32)))
    return (attn_residual, mixed.astype(jnp.bfloat16))
```

```python
import functools

import jax
import jax.numpy as jnp
from jax import lax
from jax.experimental import pallas as pl
from jax.experimental.pallas import tpu as pltpu
from jax.sharding import PartitionSpec as P

score_scale = 192.0 ** (-0.5)
log2_e = 1.4426950408889634
floor_score = -1e30
norm_eps = 1e-06
never = 1 << 30
head_group = 8
head_chunks = 2


def attention_body(q_lat, q_rope, keys, key_pos, query_pos, w_uv, out):
    lat = w_uv.shape[1]
    heads, value = w_uv.shape[0], w_uv.shape[2]
    rope = q_rope.shape[1] // heads
    tokens = q_lat.shape[0]
    queries = jnp.concatenate([q_lat[:, h * lat : (h + 1) * lat] for h in range(heads)], axis=0)
    ropes = jnp.concatenate([q_rope[:, h * rope : (h + 1) * rope] for h in range(heads)], axis=0)
    contract = (((1,), (1,)), ((), ()))
    scores = lax.dot_general(
        queries, keys[:, :lat], contract, preferred_element_type=jnp.float32
    ) + lax.dot_general(
        ropes, keys[:, lat : lat + rope], contract, preferred_element_type=jnp.float32
    )
    visible = key_pos[...] <= query_pos[...]
    scores = jnp.where(
        visible[None], scores.reshape(heads, tokens, scores.shape[1]), floor_score
    ).reshape(heads * tokens, scores.shape[1])
    top = jnp.max(scores, axis=1, keepdims=True)
    weights = jnp.exp2((scores - top) * (score_scale * log2_e))
    total = jnp.sum(weights, axis=1, keepdims=True)
    mixed = jnp.dot(weights.astype(jnp.bfloat16), keys[:, :lat], preferred_element_type=jnp.float32)
    latent = (mixed / total).astype(jnp.bfloat16)
    for h in range(heads):
        out[:, h * value : (h + 1) * value] = jnp.dot(
            latent[h * tokens : (h + 1) * tokens], w_uv[h], preferred_element_type=jnp.float32
        ).astype(out.dtype)


def attention(chunk, chunks, q_lat, q_rope, keys, key_pos, query_pos, w_uv):
    heads, lat, value = w_uv.shape
    tokens = q_lat.shape[0]
    rope = q_rope.shape[1] // heads
    count = heads // chunks
    group = min(head_group, count)
    steps = count // group
    first = chunk * steps
    n_keys, width = keys.shape
    whole = lambda g: (0, 0)
    rows = tokens * count
    return pl.pallas_call(
        attention_body,
        name="attention",
        out_shape=jax.ShapeDtypeStruct((tokens, count * value), jnp.bfloat16),
        grid=(steps,),
        in_specs=[
            pl.BlockSpec((tokens, group * lat), lambda g: (0, first + g)),
            pl.BlockSpec((tokens, group * rope), lambda g: (0, first + g)),
            pl.BlockSpec((n_keys, width), whole),
            pl.BlockSpec((1, n_keys), whole),
            pl.BlockSpec((tokens, 1), whole),
            pl.BlockSpec((group, lat, value), lambda g: (first + g, 0, 0)),
        ],
        out_specs=pl.BlockSpec((tokens, group * value), lambda g: (0, g)),
        cost_estimate=pl.CostEstimate(
            flops=2 * rows * n_keys * (width + lat) + 2 * rows * lat * value,
            bytes_accessed=2 * (rows * (lat + rope) + n_keys * width + count * lat * value),
            transcendentals=rows * n_keys,
        ),
    )(q_lat, q_rope, keys, key_pos, query_pos, w_uv)


def dot32(a, b):
    return jnp.dot(a, b, preferred_element_type=jnp.float32)


def bf(x):
    return x.astype(jnp.bfloat16)


def on_device(
    q_lat,
    q_rope,
    cache_lat,
    cache_rope,
    tool_lat,
    tool_rope,
    offset,
    suf_lat,
    suf_rope,
    w_uv,
    w_out,
    resid,
    routes,
    probs,
    w_gate,
    w_up,
    w_down,
):
    n_seq, n_exp = lax.axis_size("seq"), lax.axis_size("expert")
    n_chip = n_exp // 2
    seq, exp = lax.axis_index("seq"), lax.axis_index("expert")
    core, chip = exp % 2, exp // 2
    ring_pairs = [(j, (j + 1) % n_seq) for j in range(n_seq)]
    core_pairs = [(j, j ^ 1) for j in range(n_exp)]

    def ring(x):
        return lax.ppermute(x, "seq", ring_pairs)

    def swap(x):
        return lax.ppermute(x, "expert", core_pairs)

    def chip_shift(x, d):
        return lax.ppermute(x, "expert", [(j, (j + 2 * d) % n_exp) for j in range(n_exp)])

    ctx_dev, tool_dev, query_dev = cache_lat.shape[0], tool_lat.shape[0], q_lat.shape[0]
    rope = cache_rope.shape[1]
    pad = (-(cache_lat.shape[1] + rope)) % 128

    def joined(lat, rope_part):
        return jnp.concatenate(
            [lat, rope_part, jnp.zeros((lat.shape[0], pad), lat.dtype)], axis=1
        )

    local = jnp.concatenate(
        [joined(cache_lat, cache_rope), joined(tool_lat, tool_rope), joined(suf_lat, suf_rope)],
        axis=0,
    )
    block = local.shape[0]
    half = block // 2
    mine = lax.dynamic_slice_in_dim(local, core * half, half, axis=0)
    pieces, rows, owners = [local], [jnp.arange(block)], [jnp.full((block,), seq)]
    for k in range(1, n_seq):
        mine = ring(mine)
        other = swap(mine)
        owner = (seq - k) % n_seq
        pieces += [mine, other]
        rows += [core * half + jnp.arange(half), (1 - core) * half + jnp.arange(half)]
        owners += [jnp.full((half,), owner)] * 2
    keys = jnp.concatenate(pieces, axis=0)
    row, owner = jnp.concatenate(rows), jnp.concatenate(owners)
    start = offset[0]
    ctx_row = owner * ctx_dev + row
    tool_row = owner * tool_dev + row - ctx_dev
    replaced = (ctx_row >= start) & (ctx_row - start < tool_dev * n_seq)
    placed = (tool_row + start >= 0) & (tool_row + start < ctx_dev * n_seq)
    key_pos = jnp.where(
        row < ctx_dev,
        jnp.where(replaced, never, -1),
        jnp.where(
            row < ctx_dev + tool_dev,
            jnp.where(placed, -1, never),
            owner * query_dev + row - ctx_dev - tool_dev,
        ),
    ).astype(jnp.int32)[None, :]
    query_pos = (seq * query_dev + jnp.arange(query_dev, dtype=jnp.int32))[:, None]

    tok_dev = resid.shape[0]
    route_weight = 2.5 * probs / jnp.sum(probs, axis=1, keepdims=True)
    chosen = routes[None, :, :] == jnp.arange(n_exp * w_gate.shape[0], dtype=jnp.int32)[:, None, None]
    table = jnp.sum(jnp.where(chosen, route_weight[None, :, :], 0.0), axis=2)
    tables = jnp.stack([table] + [chip_shift(table, d) for d in range(1, n_chip)])
    tables = jnp.stack([tables, swap(tables)])
    weight = lax.dynamic_index_in_dim(tables, exp, axis=2, keepdims=False).reshape(-1)

    parts = [None] * n_seq
    k_rows = w_out.shape[0] // head_chunks
    for chunk in range(head_chunks):
        values = attention(chunk, head_chunks, q_lat, q_rope, keys, key_pos, query_pos, w_uv)
        w_part = w_out[chunk * k_rows : (chunk + 1) * k_rows]
        for k in range(n_seq):
            product = dot32(values, w_part)
            parts[k] = product if parts[k] is None else parts[k] + product
            if k + 1 < n_seq:
                values = ring(values)
    stack = jnp.concatenate([bf(p) for p in parts], axis=0)

    def token_block(d, m):
        b = 2 * ((chip - d) % n_chip) + (core ^ m)
        at = b * tok_dev
        position = ((seq - at // query_dev) % n_seq) * query_dev + at % query_dev
        return lax.dynamic_slice_in_dim(stack, position, tok_dev, axis=0)

    away = jnp.stack([token_block(d, 1) for d in range(n_chip)])
    here = jnp.stack([token_block(d, 0) for d in range(n_chip)])
    here = here.astype(jnp.float32) + swap(away).astype(jnp.float32)
    attn_sum = here[0]
    for d in range(1, n_chip):
        attn_sum = attn_sum + chip_shift(bf(here[d]), -d).astype(jnp.float32)
    attn_residual = bf(resid.astype(jnp.float32) + attn_sum)

    columns = resid.shape[1]
    gate = up = squares = 0.0
    own = attn_residual
    for k in range(n_seq):
        near = jnp.concatenate([own] + [chip_shift(own, d) for d in range(1, n_chip)], axis=0)
        stream = jnp.concatenate([near, swap(near)], axis=0)
        at = ((seq - k) % n_seq) * columns
        gate = gate + dot32(stream, lax.dynamic_slice_in_dim(w_gate[0], at, columns, axis=0))
        up = up + dot32(stream, lax.dynamic_slice_in_dim(w_up[0], at, columns, axis=0))
        wide = stream.astype(jnp.float32)
        squares = squares + jnp.sum(wide * wide, axis=1, keepdims=True)
        if k + 1 < n_seq:
            own = ring(own)
    scale = lax.rsqrt(squares / (columns * n_seq) + norm_eps)
    inner = bf(jax.nn.silu(gate * scale) * (up * scale) * weight[:, None])

    n_near = n_chip * tok_dev
    carried = None
    for k in range(1, n_seq + 1):
        at = ((seq - k) % n_seq) * columns
        out = dot32(inner, lax.dynamic_slice_in_dim(w_down[0], at, columns, axis=1))
        near = out[:n_near] + swap(bf(out[n_near:])).astype(jnp.float32)
        total = near[:tok_dev]
        for d in range(1, n_chip):
            total = total + chip_shift(bf(near[d * tok_dev : (d + 1) * tok_dev]), -d).astype(
                jnp.float32
            )
        if carried is not None:
            total = total + carried.astype(jnp.float32)
        if k < n_seq:
            carried = ring(bf(total))
    return (attn_residual, bf(total))


def solution(mesh):
    placed = (
        P(("groups", "seq"), "expert"),
        P(("groups", "seq"), "expert"),
        P(("groups", "seq"), None),
        P(("groups", "seq"), None),
        P(("groups", "seq"), None),
        P(("groups", "seq"), None),
        P("groups"),
        P(("groups", "seq"), None),
        P(("groups", "seq"), None),
        P("expert", None, None),
        P("expert", "seq"),
        P(("groups", "expert"), "seq"),
        P(("groups", "expert"), None),
        P(("groups", "expert"), None),
        P("expert", None, "seq"),
        P("expert", None, "seq"),
        P("expert", "seq", None),
    )
    return jax.shard_map(
        on_device,
        mesh=mesh,
        in_specs=placed,
        out_specs=(P(("groups", "expert"), "seq"), P(("groups", "expert"), "seq")),
        check_vma=False,
    )
```
